32 devices in a mesh: grp: 4 (over z), sub: 4 (over y, x), dev: 2 (over core).
Axes of the slice: x: 2, y: 2, z: 4, core: 2. Of those that a mesh axis runs over, the one named last changes fastest.
Arguments:
- queries: bfloat16 [4, 8, 512, 1024], P('grp', ('sub', 'dev')), may hold values from -8 to 8
- cached: bfloat16 [4, 8, 4096, 256], P('grp', ('sub', 'dev')), may hold values from -4.5 to 4.5
- new_entries: bfloat16 [4, 8, 512, 256], P('grp', ('sub', 'dev')), may hold values from -4.5 to 4.5
- lengths: int32 [8], P(('sub', 'dev')), may hold values from 1024 to 4096
- residual: bfloat16 [8, 512, 2048], P(('sub', 'dev'), 'grp'), may hold values from -6 to 6
- w_out: bfloat16 [4096, 2048], P('grp'), may hold values from -0.1875 to 0.1875
- norm_gain: float32 [2048], replicated, may hold values from 0.5 to 1.5
- w_gate_up: bfloat16 [32, 2048, 1536], P(('grp', 'sub', 'dev')), may hold values from -0.125 to 0.125
- w_down: bfloat16 [32, 768, 2048], P(('grp', 'sub', 'dev')), may hold values from -0.21875 to 0.21875
- routes: int32 [8, 512, 8], P(('sub', 'dev'), 'grp'), may hold values from 0 to 31, all different within a row; in each aligned block of 128 rows (0 to 127, 128 to 255, ..., all dimensions but the last counted through in order) at most 48 rows name the same one
- gate_codes: int32 [8, 512, 8], P(('sub', 'dev'), 'grp'), may hold values from 1 to 16
Outputs:
- attn_out: bfloat16 [8, 512, 2048], P(('sub', 'dev'), 'grp')
- mixed: bfloat16 [8, 512, 2048], P(('sub', 'dev'), 'grp')
The draws below stay inside these ranges and needn't reach their ends.
Inputs may be any that keep to these rules, and one draw needn't show every extreme that they name: `routes`: each row names 8 different experts; within the rows of one device (aligned blocks of 128 rows in the order of requests, then rows) no expert is named by more than 48 rows.
All inputs are finite; a program needn't handle non-finite values.
Results may differ from the reference program's by a relative error of at most 0.0052.
Values may be sent and summed in bfloat16 or wider, within the bound.
No kernel may reach another device: no remote copies, remote signals or barrier semaphores. Data moves between devices by JAX's collectives and lax.ppermute only.
A program may use at most 128 MiB of HBM per device.

```python
import math
import jax
import jax.numpy as jnp
import numpy as np
from jax import lax

D = 2048
FF = 768
KVH = 4
HD = 128
TOP = 8
CACHE = 4096
ROWS = 512
GQ = 8
FEAT = 4096
EXPERTS = 32
REQS = 8
MOST = 48
N_GRP = 4
DEVICES = 32


def draw_queries(key, part):
    inner = jax.random.fold_in(key, 11)
    shape = (KVH, REQS, ROWS, GQ * HD)
    values = jnp.clip(2.5 * jax.random.normal(inner, shape, jnp.float32), -8.0, 8.0)
    return values.astype(jnp.bfloat16)


def draw_cached(key, part):
    inner = jax.random.fold_in(key, 23)
    shape = (KVH, REQS, CACHE, 2 * HD)
    values = jnp.clip(jax.random.normal(inner, shape, jnp.float32), -4.5, 4.5)
    return values.astype(jnp.bfloat16)


def set_ends(values, own_key, smallest, top_value):
    longest = values.shape.index(max(values.shape))
    spots = []
    for shift in (0, 1):
        where = [jax.random.randint(jax.random.fold_in(own_key, axis), (), 0, length) for axis, length in enumerate(values.shape)]
        where[longest] = (where[longest] + shift) % values.shape[longest]
        spots.append(tuple(where))
    return values.at[spots[0]].set(smallest).at[spots[1]].set(top_value)


def steps_of(key, shape, shards, least, high):
    loudness = 1.0
    for dim, blocks in shards:
        draws = jax.random.uniform(jax.random.fold_in(jax.random.fold_in(key, 6), dim), (blocks,), jnp.float32, least / len(shards), high / len(shards))
        loudness = loudness * jnp.repeat(jnp.exp(draws), shape[dim] // blocks).reshape((-1,) + (1,) * (len(shape) - 1 - dim))
    return loudness


def assign_block(own_key, own, number, rows, count, top, most, slope):
    sequence = jax.random.permutation(own_key, count)
    heavy_load, common = load_shares(count, rows * top, most, slope, True), load_shares(count, rows * top, most, slope, False)
    places = jnp.arange(count)

    def named(sizes, offset_by):
        used = int((sizes > 0).sum())
        fixed = max(1, used // 4)
        passed = fixed + (places - fixed + offset_by * (used - fixed)) % max(1, count - fixed)
        return jnp.zeros((count,), jnp.int32).at[sequence[jnp.where(places < fixed, places, passed)]].set(jnp.asarray(sizes, jnp.int32))

    sizes = jnp.where(number % 4 == 0, named(heavy_load, number // 4), named(common, number - number // 4 - 1))
    mixed = jax.random.permutation(jax.random.fold_in(own, 3), count)
    source_of, receiver = mixed[0:count // 2 * 2:2], mixed[1:count // 2 * 2:2]
    room = jnp.minimum(sizes[source_of] - 1, most - sizes[receiver]) // 2
    room = jnp.where((source_of == sequence[0]) | (receiver == sequence[0]) | (sizes[receiver] == 0), 0, jnp.maximum(room, 0))
    passed = jax.random.randint(jax.random.fold_in(own, 4), (count // 2,), 0, 1 << 20) % (room + 1)
    sizes = sizes.at[source_of].add(-passed).at[receiver].add(passed)
    items = jnp.searchsorted(jnp.cumsum(sizes), jnp.arange(rows * top), side="right").astype(jnp.int32)
    grid = items.reshape(top, rows).T
    grid = grid[jax.random.permutation(jax.random.fold_in(own, 1), rows)]
    offset_by = jax.random.randint(jax.random.fold_in(own, 2), (rows, 1), 0, top)
    return jnp.take_along_axis(grid, (jnp.arange(top)[None, :] + offset_by) % top, axis=1)


def load_shares(number_of, total, most, lean, full):
    portions = [(1 << 20) // math.isqrt(grade ** lean) + 1 for grade in range(1, number_of + 1)]
    largest = most if full else min(most, max(-(-total // number_of), total * portions[0] // sum(portions)))
    least = 1 if total - largest >= number_of - 1 else 0
    counts, rest = [largest] + [least] * (number_of - 1), total - largest - least * (number_of - 1)
    while rest > 0:
        candidates = [i for i in range(1, number_of) if counts[i] < largest] or [i for i in range(1, number_of) if counts[i] < most]
        pool, budget = sum([portions[i] for i in candidates]), rest
        for i in candidates:
            more = min(most - counts[i], max(1, budget * portions[i] // pool), rest)
            counts[i] = counts[i] + more
            rest = rest - more
    return np.array(counts)


def normal_values(key, dims, deviation, reach, pieces=(), kind=jnp.bfloat16):
    result = deviation * jax.random.normal(key, dims, jnp.float32)
    if pieces:
        result = result * steps_of(key, dims, pieces, -0.22, 0.18)
    return jnp.clip(result, -reach, reach).astype(kind)


def setup_inputs(seed: int = 0) -> dict:
    splits = jax.random.split(jax.random.key(seed), 12)
    queries = draw_queries(jax.random.fold_in(splits[11], 71), 0)
    cached = draw_cached(jax.random.fold_in(splits[11], 71), 0)
    new_entries = normal_values(splits[2], (KVH, REQS, ROWS, 2 * HD), 1.0, 4.5, ((0, 4), (1, 8)))
    lengths = set_ends(jax.random.randint(splits[3], (REQS,), CACHE // 4, CACHE + 1), jax.random.fold_in(splits[3], 1), CACHE // 4, CACHE).astype(jnp.int32)
    residual = normal_values(splits[4], (REQS, ROWS, D), 1.0, 6.0, ((0, 8), (1, 4)))
    w_out = normal_values(splits[5], (FEAT, D), (GQ * HD) ** -0.5, 0.1875, ((0, 4),))
    norm_gain = jnp.clip(1.0 + 0.1 * jax.random.normal(splits[6], (D,), jnp.float32), 0.5, 1.5)
    w_gate_up = normal_values(splits[7], (EXPERTS, D, 2 * FF), D ** -0.5, 0.125, ((0, 32),))
    w_down = normal_values(splits[8], (EXPERTS, FF, D), FF ** -0.5, 0.21875, ((0, 32),))
    routes_keys = jax.random.split(jax.random.fold_in(splits[9], 1), REQS * ROWS // (ROWS // N_GRP))
    routes_turns = jax.random.permutation(jax.random.fold_in(splits[9], 3), REQS * ROWS // (ROWS // N_GRP))
    routes = jax.vmap(lambda own, number: assign_block(jax.random.fold_in(splits[9], 2), own, number, ROWS // N_GRP, EXPERTS, TOP, MOST, 2))(routes_keys, routes_turns).reshape((REQS, ROWS, TOP))
    gate_codes = set_ends(jax.random.randint(splits[10], (REQS, ROWS, TOP), 1, 17), jax.random.fold_in(splits[10], 1), 1, 16).astype(jnp.int32)
    return {"queries": queries, "cached": cached, "new_entries": new_entries, "lengths": lengths, "residual": residual, "w_out": w_out, "norm_gain": norm_gain, "w_gate_up": w_gate_up, "w_down": w_down, "routes": routes, "gate_codes": gate_codes}


def attend(query_rows, cached_rows, entry_rows, length):
    head_width = cached_rows.shape[1] // 2
    stored = cached_rows.shape[0]
    span_len = entry_rows.shape[0]
    key_rows = jnp.concatenate([cached_rows[:, :head_width], entry_rows[:, :head_width]], axis=0)
    value_rows = jnp.concatenate([cached_rows[:, head_width:], entry_rows[:, head_width:]], axis=0)
    position = jnp.arange(stored + span_len, dtype=jnp.int32)[None, :]
    row_index = jnp.arange(span_len, dtype=jnp.int32)[:, None]
    visible = jnp.where(position < stored, position < length, position - stored <= row_index)
    head_queries = query_rows.reshape(span_len, -1, head_width).transpose(1, 0, 2)

    def one_head(head_rows):
        scores = jnp.dot(head_rows, key_rows.T, preferred_element_type=jnp.float32) * head_width ** (-0.5)
        scores = jnp.where(visible, scores, -1e+30)
        row_peak = lax.optimization_barrier(jnp.max(scores, axis=1, keepdims=True))
        exponent = jnp.exp(scores - row_peak)
        totals = lax.optimization_barrier(jnp.sum(exponent, axis=1, keepdims=True))
        weighted = jnp.dot(exponent.astype(jnp.bfloat16), value_rows, preferred_element_type=jnp.float32)
        return (weighted / totals).astype(jnp.bfloat16)
    outputs = lax.map(one_head, head_queries)
    return outputs.transpose(1, 0, 2).reshape(span_len, -1)

def reference(queries, cached, new_entries, lengths, residual, w_out, norm_gain, w_gate_up, w_down, routes, gate_codes):
    pair_count = KVH * REQS
    query_pairs = queries.reshape(pair_count, ROWS, -1)
    cache_pairs = cached.reshape(pair_count, CACHE, -1)
    entry_pairs = new_entries.reshape(pair_count, ROWS, -1)
    pair_lengths = jnp.tile(lengths, KVH).astype(jnp.int32)
    attended = lax.map(lambda packed: attend(packed[0], packed[1], packed[2], packed[3]), (query_pairs, cache_pairs, entry_pairs, pair_lengths))
    attended = attended.reshape(KVH, REQS * ROWS, -1)
    head_feat = attended.shape[2]
    attn_sum = jnp.zeros((REQS * ROWS, D), jnp.float32)
    for head_index in range(KVH):
        block = w_out[head_index * head_feat:(head_index + 1) * head_feat]
        attn_sum = attn_sum + jnp.dot(attended[head_index], block, preferred_element_type=jnp.float32)
    attn_out = attn_sum.astype(jnp.bfloat16).reshape(REQS, ROWS, D)
    state = residual.reshape(REQS * ROWS, D).astype(jnp.float32) + attn_sum
    scale_inv = lax.rsqrt(lax.optimization_barrier(jnp.mean(state * state, axis=1, keepdims=True)) + 1e-06)
    normed = (state * scale_inv * norm_gain.astype(jnp.float32)[None, :]).astype(jnp.bfloat16)
    codes_float = gate_codes.astype(jnp.float32)
    route_weight = codes_float / lax.optimization_barrier(jnp.sum(codes_float, axis=-1, keepdims=True))
    flat_routes = routes.reshape(-1).astype(jnp.int32)
    flat_weight = route_weight.reshape(-1)
    limit = DEVICES * MOST

    def per_expert(total, expert_id):
        chosen = flat_routes == expert_id
        hits = jnp.nonzero(chosen, size=limit, fill_value=0)[0].astype(jnp.int32)
        live = jnp.arange(limit, dtype=jnp.int32) < jnp.sum(chosen.astype(jnp.int32))
        token_ids = (hits // TOP).astype(jnp.int32)
        picked = normed[token_ids]
        projected = jnp.dot(picked, w_gate_up[expert_id], preferred_element_type=jnp.float32)
        expert_hidden = (jax.nn.silu(projected[:, :FF]) * projected[:, FF:]).astype(jnp.bfloat16)
        expert_out = lax.optimization_barrier(jnp.dot(expert_hidden, w_down[expert_id], preferred_element_type=jnp.float32).astype(jnp.bfloat16))
        weight = jnp.where(live, flat_weight[hits], 0.0)
        total = total.at[token_ids].add(expert_out.astype(jnp.float32) * weight[:, None])
        return (total, None)
    moe_total, _ = lax.scan(per_expert, jnp.zeros((REQS * ROWS, D), jnp.float32), jnp.arange(EXPERTS, dtype=jnp.int32))
    mixed = (state + moe_total).astype(jnp.bfloat16).reshape(REQS, ROWS, D)
    return (attn_out, mixed)
```

```python
import functools

import jax
import jax.numpy as jnp
from jax import lax
from jax.experimental import pallas as pl
from jax.experimental.pallas import tpu as pltpu
from jax.sharding import PartitionSpec as P


TOP = 8
LOG2E = 1.4426950408889634
NEG = -1e30
MIB = 1024 * 1024


def _nt(a, b):
    return lax.dot_general(a, b, (((1,), (1,)), ((), ())), preferred_element_type=jnp.float32)


def _attend_kernel(
    meta_ref, q_ref, cached_ref, entry_ref, w_ref, *refs, block, tile, count
):
    outs = refs[:count]
    q_buf, stored, entries, w_buf, stacked, peak, acc, attended, sems = refs[count:]
    feat = attended.shape[1]
    rows = attended.shape[0] // count
    head = stored.shape[1] // 2
    heads = feat // head
    blocks = stored.shape[0] // block
    length = meta_ref[0]
    scale = head ** (-0.5) * LOG2E
    first_rows = [pl.multiple_of(meta_ref[1 + k] * rows, rows) for k in range(count)]

    def load(i):
        at = pl.ds(pl.multiple_of(i * block, block), block)
        return pltpu.make_async_copy(cached_ref.at[at, :], stored.at[at, :], sems.at[2 + count + i])

    q_copies = [
        pltpu.make_async_copy(
            q_ref.at[pl.ds(first_rows[k], rows), :], q_buf.at[k * rows : (k + 1) * rows, :], sems.at[2 + k]
        )
        for k in range(count)
    ]
    entry_copy = pltpu.make_async_copy(entry_ref, entries, sems.at[0])
    w_copy = pltpu.make_async_copy(w_ref, w_buf, sems.at[1])
    for copy in q_copies:
        copy.start()
    entry_copy.start()
    for i in range(blocks):
        load(i).start()
    w_copy.start()
    for k in range(count):
        q_copies[k].wait()
        for h in range(heads):
            at = (k * heads + h) * rows
            stacked[at : at + rows, :] = q_buf[k * rows : (k + 1) * rows, h * head : (h + 1) * head]

    def visit(pairs, mask_of, initial):
        keys = pairs[:, :head]
        size = pairs.shape[0]
        values = jnp.concatenate([pairs[:, head:], jnp.ones((size, head), jnp.bfloat16)], axis=1)
        for t in range(count * heads * rows // tile):
            at = slice(t * tile, (t + 1) * tile)
            scores = _nt(stacked[at, :], keys) * scale
            if mask_of is not None:
                scores = jnp.where(mask_of(size, t * tile // (heads * rows)), scores, NEG)
            top = jnp.max(scores, axis=1, keepdims=True)
            if initial:
                new = jnp.broadcast_to(top, (tile, head))
            else:
                old = peak[at, :]
                new = jnp.maximum(old, top)
            exponent = jnp.exp2(scores - new[:, :1]).astype(jnp.bfloat16)
            part = jnp.dot(exponent, values, preferred_element_type=jnp.float32)
            if not initial:
                shrink = jnp.exp2(old - new)
                part = part + acc[at, :] * jnp.concatenate([shrink, shrink], axis=1)
            acc[at, :] = part
            peak[at, :] = new

    def span_mask(size, k):
        own = first_rows[k] + lax.broadcasted_iota(jnp.int32, (tile, size), 0) % rows
        return lax.broadcasted_iota(jnp.int32, (tile, size), 1) <= own

    entry_copy.wait()
    visit(entries[...], span_mask, True)

    def one(i, carry):
        load(i).wait()
        start = pl.multiple_of(i * block, block)

        @pl.when(start + block <= length)
        def _():
            visit(stored[pl.ds(start, block), :], None, False)

        @pl.when((start < length) & (length < start + block))
        def _():
            def tail_mask(size, k):
                return start + lax.broadcasted_iota(jnp.int32, (tile, size), 1) < length

            visit(stored[pl.ds(start, block), :], tail_mask, False)

        return carry

    lax.fori_loop(0, blocks, one, 0)
    for k in range(count):
        for h in range(heads):
            at = slice((k * heads + h) * rows, (k * heads + h + 1) * rows)
            attended[k * rows : (k + 1) * rows, h * head : (h + 1) * head] = (
                acc[at, :head] / acc[at, head:]
            ).astype(jnp.bfloat16)
    w_copy.wait()
    total = jnp.dot(attended[...], w_buf[...], preferred_element_type=jnp.float32)
    for k, out in enumerate(outs):
        out[...] = total[k * rows : (k + 1) * rows].astype(out.dtype)


BLOCK = 2048
TILE = 128


def attend_rows(meta, queries, cached, entries, w_out, rows, dtypes):
    span, feat = queries.shape
    stored, pair = cached.shape
    head = pair // 2
    width = w_out.shape[1]
    count = len(dtypes)
    group = rows * feat // head
    stack = count * group
    block = BLOCK if stored % BLOCK == 0 else stored
    tile = TILE if group % TILE == 0 else group
    flops = 4 * stack * (stored + span) * head + 2 * count * rows * feat * width
    bf16 = jnp.bfloat16
    return pl.pallas_call(
        functools.partial(_attend_kernel, block=block, tile=tile, count=count),
        out_shape=tuple(jax.ShapeDtypeStruct((rows, width), dtype) for dtype in dtypes),
        in_specs=[pl.BlockSpec(memory_space=pltpu.SMEM)] + [pl.BlockSpec(memory_space=pl.ANY)] * 4,
        out_specs=(pl.BlockSpec(memory_space=pltpu.VMEM),) * count,
        scratch_shapes=[
            pltpu.VMEM((count * rows, feat), bf16),
            pltpu.VMEM((stored, pair), bf16),
            pltpu.VMEM((span, pair), bf16),
            pltpu.VMEM((feat, width), bf16),
            pltpu.VMEM((stack, head), bf16),
            pltpu.VMEM((stack, head), jnp.float32),
            pltpu.VMEM((stack, pair), jnp.float32),
            pltpu.VMEM((count * rows, feat), bf16),
            pltpu.SemaphoreType.DMA((2 + count + stored // block,)),
        ],
        compiler_params=pltpu.CompilerParams(vmem_limit_bytes=60 * MIB),
        cost_estimate=pl.CostEstimate(
            flops=2 * flops,
            bytes_accessed=2 * (stored * pair + feat * width + count * rows * (feat + width)),
            transcendentals=stack * (stored + span),
        ),
        name="attend_rows",
    )(meta, queries, cached, entries, w_out)


def _slots(place_ref, index, capacity, rows, weights=None):
    place = place_ref[index : index + 1, :]
    hit = lax.broadcasted_iota(jnp.int32, (capacity, rows), 0).astype(jnp.float32) == place
    if weights is None:
        return jnp.where(hit, 1.0, 0.0).astype(jnp.bfloat16)
    return jnp.where(hit, weights[index : index + 1, :], 0.0).astype(jnp.bfloat16)


def _pick_kernel(place_ref, *refs, capacity):
    own_ref, other_ref = refs[4:]
    rows = place_ref.shape[1]
    for j in range(4):
        own = _slots(place_ref, 2 * j, capacity, rows)
        other = _slots(place_ref, 2 * j + 1, capacity, rows)
        pick = jnp.concatenate([own, other], axis=0)
        found = jnp.dot(pick, refs[j][...], preferred_element_type=jnp.float32).astype(jnp.bfloat16)
        own_ref[j * capacity : (j + 1) * capacity, :] = found[:capacity]
        other_ref[j * capacity : (j + 1) * capacity, :] = found[capacity:]


def pick_rows(place, pieces, capacity):
    rows, width = place.shape[1], pieces[0].shape[1]
    shape = jax.ShapeDtypeStruct((4 * capacity, width), jnp.bfloat16)
    return pl.pallas_call(
        functools.partial(_pick_kernel, capacity=capacity),
        out_shape=(shape, shape),
        compiler_params=pltpu.CompilerParams(vmem_limit_bytes=16 * MIB),
        cost_estimate=pl.CostEstimate(
            flops=16 * capacity * rows * width, bytes_accessed=2 * 4 * width * (rows + 2 * capacity), transcendentals=0
        ),
        name="pick_rows",
    )(place, *pieces)


def _blend_kernel(place_ref, code_ref, own_ref, other_ref, *outs, capacity):
    rows = place_ref.shape[1]
    for j in range(4):
        own = _slots(place_ref, 2 * j, capacity, rows, code_ref)
        other = _slots(place_ref, 2 * j + 1, capacity, rows, code_ref)
        pick = jnp.concatenate([own, other], axis=0)
        at = slice(j * capacity, (j + 1) * capacity)
        made = jnp.concatenate([own_ref[at, :], other_ref[at, :]], axis=0)
        outs[j][...] = lax.dot_general(
            pick, made, (((0,), (0,)), ((), ())), preferred_element_type=jnp.float32
        ).astype(jnp.bfloat16)


def blend_rows(place, codes, own, other, capacity):
    width = own.shape[1]
    rows = place.shape[1]
    return pl.pallas_call(
        functools.partial(_blend_kernel, capacity=capacity),
        out_shape=(jax.ShapeDtypeStruct((rows, width), jnp.bfloat16),) * 4,
        compiler_params=pltpu.CompilerParams(vmem_limit_bytes=16 * MIB),
        cost_estimate=pl.CostEstimate(
            flops=16 * capacity * rows * width, bytes_accessed=2 * 4 * width * (rows + 2 * capacity), transcendentals=0
        ),
        name="blend_rows",
    )(place, codes, own, other)


def _expert_kernel(*refs, count):
    ins, (both_ref, down_ref) = refs[:count], refs[count : count + 2]
    outs, (rows, acc) = refs[count + 2 : -2], refs[-2:]
    size = ins[0].shape[0]
    hidden = down_ref.shape[1]
    part = 256 if hidden % 256 == 0 else hidden
    for k, ref in enumerate(ins):
        rows[k * size : (k + 1) * size, :] = ref[...]

    def partial_sum(c):
        start = c * part
        gate = jnp.dot(rows[...], both_ref[0, :, pl.ds(start, part)], preferred_element_type=jnp.float32)
        up = jnp.dot(rows[...], both_ref[0, :, pl.ds(hidden + start, part)], preferred_element_type=jnp.float32)
        mid = (gate / (1.0 + jnp.exp(-gate)) * up).astype(jnp.bfloat16)
        return jnp.dot(mid, down_ref[0, pl.ds(start, part), :], preferred_element_type=jnp.float32)

    steps = hidden // part
    acc[...] = partial_sum(0)

    for c in range(1, steps):
        total = acc[...] + partial_sum(c)
        if c < steps - 1:
            acc[...] = total
        else:
            for k, out in enumerate(outs):
                out[...] = total[k * size : (k + 1) * size].astype(jnp.bfloat16)
    if steps == 1:
        for k, out in enumerate(outs):
            out[...] = acc[k * size : (k + 1) * size].astype(jnp.bfloat16)


def expert_rows(pieces, w_gate_up, w_down):
    count, width = pieces[0].shape
    number = len(pieces)
    hidden = w_down.shape[1]
    return pl.pallas_call(
        functools.partial(_expert_kernel, count=number),
        out_shape=(jax.ShapeDtypeStruct((count, width), jnp.bfloat16),) * number,
        scratch_shapes=[
            pltpu.VMEM((number * count, width), jnp.bfloat16),
            pltpu.VMEM((number * count, width), jnp.float32),
        ],
        compiler_params=pltpu.CompilerParams(vmem_limit_bytes=40 * MIB),
        cost_estimate=pl.CostEstimate(
            flops=6 * number * count * width * hidden,
            bytes_accessed=2 * (3 * width * hidden + 2 * number * count * width),
            transcendentals=number * count * hidden,
        ),
        name="expert_rows",
    )(*pieces, w_gate_up, w_down)


def _norm_kernel(own_ref, *refs, count):
    got, (residual_ref, gain_ref, out_ref, state_ref, normed_ref) = refs[:count], refs[count:]
    total = own_ref[...].astype(jnp.float32)
    for ref in got:
        total = total + ref[...].astype(jnp.float32)
    out_ref[...] = total.astype(jnp.bfloat16)
    state = residual_ref[...].astype(jnp.float32) + total
    state_ref[...] = state
    scale = lax.rsqrt(jnp.mean(state * state, axis=1, keepdims=True) + 1e-06)
    normed_ref[...] = (state * scale * gain_ref[...]).astype(jnp.bfloat16)


def norm_rows(own, got, residual, gain):
    rows, width = own.shape
    like = lambda dtype: jax.ShapeDtypeStruct((rows, width), dtype)
    return pl.pallas_call(
        functools.partial(_norm_kernel, count=len(got)),
        out_shape=(like(jnp.bfloat16), like(jnp.float32), like(jnp.bfloat16)),
        compiler_params=pltpu.CompilerParams(vmem_limit_bytes=16 * MIB),
        cost_estimate=pl.CostEstimate(
            flops=8 * rows * width, bytes_accessed=rows * width * (14 + 2 * len(got)), transcendentals=rows
        ),
        name="norm_rows",
    )(own, *got, residual, gain[None, :])


def swap(value, axis, bit):
    size = lax.axis_size(axis)
    return lax.ppermute(value, axis, [(i, i ^ bit) for i in range(size)])


def share_codes(routes, gate_codes):
    axes = ("grp", "sub", "dev")
    devices = lax.axis_size("grp") * lax.axis_size("sub") * lax.axis_size("dev")
    hits = routes[:, :, None] == jnp.arange(devices, dtype=jnp.int32)[None, None, :]
    dense = jnp.sum(jnp.where(hits, gate_codes[:, :, None], 0), axis=1).astype(jnp.float32)
    return lax.all_to_all(dense.T, axes, split_axis=0, concat_axis=0, tiled=True)


def place_codes(mine):
    groups, subgroups, members = (lax.axis_size(a) for a in ("grp", "sub", "dev"))
    rows = mine.shape[1]
    other = swap(mine, "dev", 1)
    me = [lax.axis_index(a) for a in ("grp", "sub", "dev")]
    order = jnp.stack(
        [((me[0] ^ i) * subgroups + (me[1] ^ j)) * members + me[2] for i in range(groups) for j in range(subgroups)]
    )
    both = jnp.stack([mine[order], other[order]], axis=1).reshape(-1, rows)
    index = jnp.arange(rows, dtype=jnp.int32)
    upper = (index[:, None] <= index[None, :]).astype(jnp.float32)
    rank = jnp.dot((both > 0).astype(jnp.float32), upper, preferred_element_type=jnp.float32)
    place = jnp.where(both > 0, rank - 1.0, -1.0)
    shape = (groups, 2 * subgroups, rows)
    return place.reshape(shape), both.reshape(shape)


def column_first(i):
    return (i ^ (i >> 1)) % 2 == 1


def spread(normed):
    groups = lax.axis_size("grp")
    held = [normed] + [None] * (groups - 1)
    bit = groups // 2
    while bit:
        for i in range(0, groups, 2 * bit):
            held[i + bit] = swap(held[i], "grp", bit)
        bit //= 2
    for i, z in enumerate(held):
        x = swap(z, "sub", 1)
        y = swap(z, "sub", 2)
        far = (y, 1) if column_first(i) else (x, 2)
        held[i] = (z, x, y, swap(far[0], "sub", far[1]))
    return held


def experts(held, place, codes, w_gate_up, w_down):
    groups, subgroups, members = (lax.axis_size(a) for a in ("grp", "sub", "dev"))
    rows = place.shape[2]
    capacity = max(2, rows * TOP * 3 // (2 * groups * subgroups * members))
    f32 = lambda v: v.astype(jnp.float32)
    batch = 2 if groups % 2 == 0 else 1
    parts = [None] * groups
    for first in range(groups - batch, -1, -batch):
        pieces = []
        members_of = range(first + batch - 1, first - 1, -1)
        for i in members_of:
            own, sent = pick_rows(place[i], held[i], capacity)
            pieces += [own, swap(sent, "dev", 1)]
        made = expert_rows(pieces, w_gate_up, w_down)
        for n, i in enumerate(members_of):
            own, back = made[2 * n : 2 * n + 2]
            back = swap(back, "dev", 1)
            parts[i] = blend_rows(place[i], codes[i], own, back, capacity)
    sums = [None] * groups
    for i in range(groups - 1, -1, -1):
        sz, sx, sy, sd = parts[i]
        if column_first(i):
            sy = (f32(sy) + f32(swap(sd, "sub", 1))).astype(jnp.bfloat16)
        else:
            sx = (f32(sx) + f32(swap(sd, "sub", 2))).astype(jnp.bfloat16)
        sums[i] = f32(sz) + f32(swap(sx, "sub", 1)) + f32(swap(sy, "sub", 2))
    bit = 1
    while bit < groups:
        for i in range(groups - 2 * bit, -1, -2 * bit):
            sums[i] = sums[i] + f32(swap(sums[i + bit].astype(jnp.bfloat16), "grp", bit))
        bit *= 2
    return sums[0]


def moe_exchange(normed, routes, gate_codes, w_gate_up, w_down):
    axes = ("grp", "sub", "dev")
    devices = lax.axis_size("grp") * lax.axis_size("sub") * lax.axis_size("dev")
    own_rows, width = normed.shape
    local_experts = w_gate_up.shape[0]
    expert_total = local_experts * devices
    hidden_width = w_down.shape[1]
    capacity = max(2, own_rows * TOP * 3 // (2 * expert_total))
    codes_float = gate_codes.astype(jnp.float32)
    route_weight = codes_float / jnp.sum(codes_float, axis=-1, keepdims=True)
    flat_routes = routes.reshape(-1)
    assigned = flat_routes.shape[0]
    one_hot = (flat_routes[:, None] == jnp.arange(expert_total, dtype=jnp.int32)[None, :]).astype(jnp.int32)
    earlier_hits = jnp.cumsum(one_hot, axis=0) - one_hot
    rank_within = jnp.sum(earlier_hits * one_hot, axis=1)
    slot_index = flat_routes * capacity + rank_within
    slot_token = (
        jnp.zeros((expert_total * capacity,), jnp.int32)
        .at[slot_index]
        .set(jnp.arange(assigned, dtype=jnp.int32) // TOP)
    )
    filled = jnp.zeros((expert_total * capacity,), jnp.bool_).at[slot_index].set(True)
    outgoing = jnp.where(filled[:, None], normed[slot_token], jnp.zeros((), jnp.bfloat16))
    received = lax.all_to_all(outgoing.reshape(devices, -1, width), axes, split_axis=0, concat_axis=0, tiled=True)
    batches = received.reshape(devices, local_experts, capacity, width)
    projected = jnp.einsum("secd,edf->secf", batches, w_gate_up, preferred_element_type=jnp.float32)
    expert_hidden = (jax.nn.silu(projected[..., :hidden_width]) * projected[..., hidden_width:]).astype(jnp.bfloat16)
    expert_out = jnp.einsum("secf,efd->secd", expert_hidden, w_down, preferred_element_type=jnp.float32)
    produced = expert_out.astype(jnp.bfloat16).reshape(devices, -1, width)
    returned = lax.all_to_all(produced, axes, split_axis=0, concat_axis=0, tiled=True)
    picked = returned.reshape(-1, width)[slot_index].reshape(own_rows, TOP, width).astype(jnp.float32)
    return jnp.sum(picked * route_weight[:, :, None], axis=1)


def per_device(
    queries,
    cached,
    new_entries,
    lengths,
    residual,
    w_out,
    norm_gain,
    w_gate_up,
    w_down,
    routes,
    gate_codes,
    *,
    sheet,
):
    rows = residual.shape[1]
    groups = lax.axis_size("grp")
    me = lax.axis_index("grp")
    if sheet:
        mine = share_codes(routes[0], gate_codes[0])

    def attend(i):
        return attend_rows(
            jnp.stack([lengths[0], me ^ i]), queries[0, 0], cached[0, 0], new_entries[0, 0], w_out, rows,
            (jnp.bfloat16,),
        )[0]

    waiting = [[] for _ in range(groups)]
    bit = 1
    while bit < groups:
        for i in range(groups - bit, 0, -2 * bit):
            part = attend(i)
            if waiting[i]:
                part = sum((v.astype(jnp.float32) for v in waiting[i]), part.astype(jnp.float32)).astype(part.dtype)
            waiting[i - bit].append(swap(part, "grp", bit))
        bit *= 2
    own = attend(0)
    attn_out, state, normed = norm_rows(own, waiting[0], residual[0], norm_gain)
    if sheet:
        total = experts(spread(normed), *place_codes(mine), w_gate_up, w_down)
        moe_total = total / jnp.sum(gate_codes[0].astype(jnp.float32), axis=-1, keepdims=True)
    else:
        moe_total = moe_exchange(normed, routes[0], gate_codes[0], w_gate_up, w_down)
    mixed = (state + moe_total).astype(jnp.bfloat16)
    return (attn_out[None], mixed[None])


def solution(mesh):
    placed = (
        P("grp", ("sub", "dev"), None, None),
        P("grp", ("sub", "dev"), None, None),
        P("grp", ("sub", "dev"), None, None),
        P(("sub", "dev")),
        P(("sub", "dev"), "grp", None),
        P("grp", None),
        P(),
        P(("grp", "sub", "dev"), None, None),
        P(("grp", "sub", "dev"), None, None),
        P(("sub", "dev"), "grp", None),
        P(("sub", "dev"), "grp", None),
    )
    shape = mesh.shape
    sheet = shape["grp"] == 4 and shape["sub"] == 4 and shape["dev"] == 2

    def body(*args):
        return per_device(*args, sheet=sheet)

    return jax.shard_map(
        body,
        mesh=mesh,
        in_specs=placed,
        out_specs=(P(("sub", "dev"), "grp", None), P(("sub", "dev"), "grp", None)),
        check_vma=False,
    )
```

```python
import functools

import jax
import jax.numpy as jnp
from jax import lax
from jax.experimental import pallas as pl
from jax.experimental.pallas import tpu as pltpu
from jax.sharding import PartitionSpec as P


TOP = 8
LOG2E = 1.4426950408889634
NEG = -1e30
MIB = 1024 * 1024


def _nt(a, b):
    return lax.dot_general(a, b, (((1,), (1,)), ((), ())), preferred_element_type=jnp.float32)


def _attend_kernel(
    meta_ref, q_ref, cached_ref, entry_ref, w_ref, *refs, block, tile, count
):
    outs = refs[:count]
    q_buf, stored, entries, w_buf, stacked, peak, acc, attended, sems = refs[count:]
    feat = attended.shape[1]
    rows = attended.shape[0] // count
    head = stored.shape[1] // 2
    heads = feat // head
    blocks = stored.shape[0] // block
    length = meta_ref[0]
    scale = head ** (-0.5) * LOG2E
    first_rows = [pl.multiple_of(meta_ref[1 + k] * rows, rows) for k in range(count)]

    def load(i):
        at = pl.ds(pl.multiple_of(i * block, block), block)
        return pltpu.make_async_copy(cached_ref.at[at, :], stored.at[at, :], sems.at[2 + count + i])

    q_copies = [
        pltpu.make_async_copy(
            q_ref.at[pl.ds(first_rows[k], rows), :], q_buf.at[k * rows : (k + 1) * rows, :], sems.at[2 + k]
        )
        for k in range(count)
    ]
    entry_copy = pltpu.make_async_copy(entry_ref, entries, sems.at[0])
    w_copy = pltpu.make_async_copy(w_ref, w_buf, sems.at[1])
    for copy in q_copies:
        copy.start()
    entry_copy.start()
    for i in range(blocks):
        load(i).start()
    w_copy.start()
    for k in range(count):
        q_copies[k].wait()
        for h in range(heads):
            at = (k * heads + h) * rows
            stacked[at : at + rows, :] = q_buf[k * rows : (k + 1) * rows, h * head : (h + 1) * head]

    def visit(pairs, mask_of, initial):
        keys = pairs[:, :head]
        size = pairs.shape[0]
        values = jnp.concatenate([pairs[:, head:], jnp.ones((size, head), jnp.bfloat16)], axis=1)
        for t in range(count * heads * rows // tile):
            at = slice(t * tile, (t + 1) * tile)
            scores = _nt(stacked[at, :], keys) * scale
            if mask_of is not None:
                scores = jnp.where(mask_of(size, t * tile // (heads * rows)), scores, NEG)
            top = jnp.max(scores, axis=1, keepdims=True)
            if initial:
                new = jnp.broadcast_to(top, (tile, head))
            else:
                old = peak[at, :]
                new = jnp.maximum(old, top)
            exponent = jnp.exp2(scores - new[:, :1]).astype(jnp.bfloat16)
            part = jnp.dot(exponent, values, preferred_element_type=jnp.float32)
            if not initial:
                shrink = jnp.exp2(old - new)
                part = part + acc[at, :] * jnp.concatenate([shrink, shrink], axis=1)
            acc[at, :] = part
            peak[at, :] = new

    def span_mask(size, k):
        own = first_rows[k] + lax.broadcasted_iota(jnp.int32, (tile, size), 0) % rows
        return lax.broadcasted_iota(jnp.int32, (tile, size), 1) <= own

    entry_copy.wait()
    visit(entries[...], span_mask, True)

    def one(i, carry):
        load(i).wait()
        start = pl.multiple_of(i * block, block)

        @pl.when(start < length)
        def _():
            def tail_mask(size, k):
                return start + lax.broadcasted_iota(jnp.int32, (tile, size), 1) < length

            visit(stored[pl.ds(start, block), :], tail_mask, False)

        return carry

    lax.fori_loop(0, blocks, one, 0)
    for k in range(count):
        for h in range(heads):
            at = slice((k * heads + h) * rows, (k * heads + h + 1) * rows)
            attended[k * rows : (k + 1) * rows, h * head : (h + 1) * head] = (
                acc[at, :head] / acc[at, head:]
            ).astype(jnp.bfloat16)
    w_copy.wait()
    total = jnp.dot(attended[...], w_buf[...], preferred_element_type=jnp.float32)
    for k, out in enumerate(outs):
        out[...] = total[k * rows : (k + 1) * rows].astype(out.dtype)


BLOCK = 1024
TILE = 128


def attend_rows(meta, queries, cached, entries, w_out, rows, dtypes):
    span, feat = queries.shape
    stored, pair = cached.shape
    head = pair // 2
    width = w_out.shape[1]
    count = len(dtypes)
    group = rows * feat // head
    stack = count * group
    block = BLOCK if stored % BLOCK == 0 else stored
    tile = TILE if group % TILE == 0 else group
    flops = 4 * stack * (stored + span) * head + 2 * count * rows * feat * width
    bf16 = jnp.bfloat16
    return pl.pallas_call(
        functools.partial(_attend_kernel, block=block, tile=tile, count=count),
        out_shape=tuple(jax.ShapeDtypeStruct((rows, width), dtype) for dtype in dtypes),
        in_specs=[pl.BlockSpec(memory_space=pltpu.SMEM)] + [pl.BlockSpec(memory_space=pl.ANY)] * 4,
        out_specs=(pl.BlockSpec(memory_space=pltpu.VMEM),) * count,
        scratch_shapes=[
            pltpu.VMEM((count * rows, feat), bf16),
            pltpu.VMEM((stored, pair), bf16),
            pltpu.VMEM((span, pair), bf16),
            pltpu.VMEM((feat, width), bf16),
            pltpu.VMEM((stack, head), bf16),
            pltpu.VMEM((stack, head), jnp.float32),
            pltpu.VMEM((stack, pair), jnp.float32),
            pltpu.VMEM((count * rows, feat), bf16),
            pltpu.SemaphoreType.DMA((2 + count + stored // block,)),
        ],
        compiler_params=pltpu.CompilerParams(vmem_limit_bytes=60 * MIB),
        cost_estimate=pl.CostEstimate(
            flops=2 * flops,
            bytes_accessed=2 * (stored * pair + feat * width + count * rows * (feat + width)),
            transcendentals=stack * (stored + span),
        ),
        name="attend_rows",
    )(meta, queries, cached, entries, w_out)


def _slots(place_ref, index, capacity, rows, weights=None):
    place = place_ref[index : index + 1, :]
    hit = lax.broadcasted_iota(jnp.int32, (capacity, rows), 0).astype(jnp.float32) == place
    if weights is None:
        return jnp.where(hit, 1.0, 0.0).astype(jnp.bfloat16)
    return jnp.where(hit, weights[index : index + 1, :], 0.0).astype(jnp.bfloat16)


def _pick_kernel(place_ref, *refs, capacity):
    own_ref, other_ref = refs[4:]
    rows = place_ref.shape[1]
    for j in range(4):
        own = _slots(place_ref, 2 * j, capacity, rows)
        other = _slots(place_ref, 2 * j + 1, capacity, rows)
        pick = jnp.concatenate([own, other], axis=0)
        found = jnp.dot(pick, refs[j][...], preferred_element_type=jnp.float32).astype(jnp.bfloat16)
        own_ref[j * capacity : (j + 1) * capacity, :] = found[:capacity]
        other_ref[j * capacity : (j + 1) * capacity, :] = found[capacity:]


def pick_rows(place, pieces, capacity):
    rows, width = place.shape[1], pieces[0].shape[1]
    shape = jax.ShapeDtypeStruct((4 * capacity, width), jnp.bfloat16)
    return pl.pallas_call(
        functools.partial(_pick_kernel, capacity=capacity),
        out_shape=(shape, shape),
        compiler_params=pltpu.CompilerParams(vmem_limit_bytes=16 * MIB),
        cost_estimate=pl.CostEstimate(
            flops=16 * capacity * rows * width, bytes_accessed=2 * 4 * width * (rows + 2 * capacity), transcendentals=0
        ),
        name="pick_rows",
    )(place, *pieces)


def _blend_kernel(place_ref, code_ref, own_ref, other_ref, *outs, capacity):
    rows = place_ref.shape[1]
    for j in range(4):
        own = _slots(place_ref, 2 * j, capacity, rows, code_ref)
        other = _slots(place_ref, 2 * j + 1, capacity, rows, code_ref)
        pick = jnp.concatenate([own, other], axis=0)
        at = slice(j * capacity, (j + 1) * capacity)
        made = jnp.concatenate([own_ref[at, :], other_ref[at, :]], axis=0)
        outs[j][...] = lax.dot_general(
            pick, made, (((0,), (0,)), ((), ())), preferred_element_type=jnp.float32
        ).astype(jnp.bfloat16)


def blend_rows(place, codes, own, other, capacity):
    width = own.shape[1]
    rows = place.shape[1]
    return pl.pallas_call(
        functools.partial(_blend_kernel, capacity=capacity),
        out_shape=(jax.ShapeDtypeStruct((rows, width), jnp.bfloat16),) * 4,
        compiler_params=pltpu.CompilerParams(vmem_limit_bytes=16 * MIB),
        cost_estimate=pl.CostEstimate(
            flops=16 * capacity * rows * width, bytes_accessed=2 * 4 * width * (rows + 2 * capacity), transcendentals=0
        ),
        name="blend_rows",
    )(place, codes, own, other)


def _expert_kernel(*refs, count):
    ins, (both_ref, down_ref) = refs[:count], refs[count : count + 2]
    outs, (rows, acc) = refs[count + 2 : -2], refs[-2:]
    size = ins[0].shape[0]
    hidden = down_ref.shape[1]
    part = 256 if hidden % 256 == 0 else hidden
    for k, ref in enumerate(ins):
        rows[k * size : (k + 1) * size, :] = ref[...]

    def partial_sum(c):
        start = c * part
        gate = jnp.dot(rows[...], both_ref[0, :, pl.ds(start, part)], preferred_element_type=jnp.float32)
        up = jnp.dot(rows[...], both_ref[0, :, pl.ds(hidden + start, part)], preferred_element_type=jnp.float32)
        mid = (gate / (1.0 + jnp.exp(-gate)) * up).astype(jnp.bfloat16)
        return jnp.dot(mid, down_ref[0, pl.ds(start, part), :], preferred_element_type=jnp.float32)

    steps = hidden // part
    acc[...] = partial_sum(0)

    for c in range(1, steps):
        total = acc[...] + partial_sum(c)
        if c < steps - 1:
            acc[...] = total
        else:
            for k, out in enumerate(outs):
                out[...] = total[k * size : (k + 1) * size].astype(jnp.bfloat16)
    if steps == 1:
        for k, out in enumerate(outs):
            out[...] = acc[k * size : (k + 1) * size].astype(jnp.bfloat16)


def expert_rows(pieces, w_gate_up, w_down):
    count, width = pieces[0].shape
    number = len(pieces)
    hidden = w_down.shape[1]
    return pl.pallas_call(
        functools.partial(_expert_kernel, count=number),
        out_shape=(jax.ShapeDtypeStruct((count, width), jnp.bfloat16),) * number,
        scratch_shapes=[
            pltpu.VMEM((number * count, width), jnp.bfloat16),
            pltpu.VMEM((number * count, width), jnp.float32),
        ],
        compiler_params=pltpu.CompilerParams(vmem_limit_bytes=40 * MIB),
        cost_estimate=pl.CostEstimate(
            flops=6 * number * count * width * hidden,
            bytes_accessed=2 * (3 * width * hidden + 2 * number * count * width),
            transcendentals=number * count * hidden,
        ),
        name="expert_rows",
    )(*pieces, w_gate_up, w_down)


def _norm_kernel(own_ref, *refs, count):
    got, (residual_ref, gain_ref, out_ref, state_ref, normed_ref) = refs[:count], refs[count:]
    total = own_ref[...].astype(jnp.float32)
    for ref in got:
        total = total + ref[...].astype(jnp.float32)
    out_ref[...] = total.astype(jnp.bfloat16)
    state = residual_ref[...].astype(jnp.float32) + total
    state_ref[...] = state
    scale = lax.rsqrt(jnp.mean(state * state, axis=1, keepdims=True) + 1e-06)
    normed_ref[...] = (state * scale * gain_ref[...]).astype(jnp.bfloat16)


def norm_rows(own, got, residual, gain):
    rows, width = own.shape
    like = lambda dtype: jax.ShapeDtypeStruct((rows, width), dtype)
    return pl.pallas_call(
        functools.partial(_norm_kernel, count=len(got)),
        out_shape=(like(jnp.bfloat16), like(jnp.float32), like(jnp.bfloat16)),
        compiler_params=pltpu.CompilerParams(vmem_limit_bytes=16 * MIB),
        cost_estimate=pl.CostEstimate(
            flops=8 * rows * width, bytes_accessed=rows * width * (14 + 2 * len(got)), transcendentals=rows
        ),
        name="norm_rows",
    )(own, *got, residual, gain[None, :])


def swap(value, axis, bit):
    size = lax.axis_size(axis)
    return lax.ppermute(value, axis, [(i, i ^ bit) for i in range(size)])


def share_codes(routes, gate_codes):
    axes = ("grp", "sub", "dev")
    devices = lax.axis_size("grp") * lax.axis_size("sub") * lax.axis_size("dev")
    hits = routes[:, :, None] == jnp.arange(devices, dtype=jnp.int32)[None, None, :]
    dense = jnp.sum(jnp.where(hits, gate_codes[:, :, None], 0), axis=1).astype(jnp.float32)
    return lax.all_to_all(dense.T, axes, split_axis=0, concat_axis=0, tiled=True)


def place_codes(mine):
    groups, subgroups, members = (lax.axis_size(a) for a in ("grp", "sub", "dev"))
    rows = mine.shape[1]
    other = swap(mine, "dev", 1)
    me = [lax.axis_index(a) for a in ("grp", "sub", "dev")]
    order = jnp.stack(
        [((me[0] ^ i) * subgroups + (me[1] ^ j)) * members + me[2] for i in range(groups) for j in range(subgroups)]
    )
    both = jnp.stack([mine[order], other[order]], axis=1).reshape(-1, rows)
    index = jnp.arange(rows, dtype=jnp.int32)
    upper = (index[:, None] <= index[None, :]).astype(jnp.float32)
    rank = jnp.dot((both > 0).astype(jnp.float32), upper, preferred_element_type=jnp.float32)
    place = jnp.where(both > 0, rank - 1.0, -1.0)
    shape = (groups, 2 * subgroups, rows)
    return place.reshape(shape), both.reshape(shape)


def column_first(i):
    return (i ^ (i >> 1)) % 2 == 1


def spread(normed):
    groups = lax.axis_size("grp")
    held = [normed] + [None] * (groups - 1)
    bit = groups // 2
    while bit:
        for i in range(0, groups, 2 * bit):
            held[i + bit] = swap(held[i], "grp", bit)
        bit //= 2
    for i, z in enumerate(held):
        x = swap(z, "sub", 1)
        y = swap(z, "sub", 2)
        far = (y, 1) if column_first(i) else (x, 2)
        held[i] = (z, x, y, swap(far[0], "sub", far[1]))
    return held


def experts(held, place, codes, w_gate_up, w_down):
    groups, subgroups, members = (lax.axis_size(a) for a in ("grp", "sub", "dev"))
    rows = place.shape[2]
    capacity = max(2, rows * TOP * 3 // (2 * groups * subgroups * members))
    f32 = lambda v: v.astype(jnp.float32)
    batch = 2 if groups % 2 == 0 else 1
    parts = [None] * groups
    for first in range(groups - batch, -1, -batch):
        pieces = []
        members_of = range(first + batch - 1, first - 1, -1)
        for i in members_of:
            own, sent = pick_rows(place[i], held[i], capacity)
            pieces += [own, swap(sent, "dev", 1)]
        made = expert_rows(pieces, w_gate_up, w_down)
        for n, i in enumerate(members_of):
            own, back = made[2 * n : 2 * n + 2]
            back = swap(back, "dev", 1)
            parts[i] = blend_rows(place[i], codes[i], own, back, capacity)
    sums = [None] * groups
    for i in range(groups - 1, -1, -1):
        sz, sx, sy, sd = parts[i]
        if column_first(i):
            sy = (f32(sy) + f32(swap(sd, "sub", 1))).astype(jnp.bfloat16)
        else:
            sx = (f32(sx) + f32(swap(sd, "sub", 2))).astype(jnp.bfloat16)
        sums[i] = f32(sz) + f32(swap(sx, "sub", 1)) + f32(swap(sy, "sub", 2))
    bit = 1
    while bit < groups:
        for i in range(groups - 2 * bit, -1, -2 * bit):
            sums[i] = sums[i] + f32(swap(sums[i + bit].astype(jnp.bfloat16), "grp", bit))
        bit *= 2
    return sums[0]


def moe_exchange(normed, routes, gate_codes, w_gate_up, w_down):
    axes = ("grp", "sub", "dev")
    devices = lax.axis_size("grp") * lax.axis_size("sub") * lax.axis_size("dev")
    own_rows, width = normed.shape
    local_experts = w_gate_up.shape[0]
    expert_total = local_experts * devices
    hidden_width = w_down.shape[1]
    capacity = max(2, own_rows * TOP * 3 // (2 * expert_total))
    codes_float = gate_codes.astype(jnp.float32)
    route_weight = codes_float / jnp.sum(codes_float, axis=-1, keepdims=True)
    flat_routes = routes.reshape(-1)
    assigned = flat_routes.shape[0]
    one_hot = (flat_routes[:, None] == jnp.arange(expert_total, dtype=jnp.int32)[None, :]).astype(jnp.int32)
    earlier_hits = jnp.cumsum(one_hot, axis=0) - one_hot
    rank_within = jnp.sum(earlier_hits * one_hot, axis=1)
    slot_index = flat_routes * capacity + rank_within
    slot_token = (
        jnp.zeros((expert_total * capacity,), jnp.int32)
        .at[slot_index]
        .set(jnp.arange(assigned, dtype=jnp.int32) // TOP)
    )
    filled = jnp.zeros((expert_total * capacity,), jnp.bool_).at[slot_index].set(True)
    outgoing = jnp.where(filled[:, None], normed[slot_token], jnp.zeros((), jnp.bfloat16))
    received = lax.all_to_all(outgoing.reshape(devices, -1, width), axes, split_axis=0, concat_axis=0, tiled=True)
    batches = received.reshape(devices, local_experts, capacity, width)
    projected = jnp.einsum("secd,edf->secf", batches, w_gate_up, preferred_element_type=jnp.float32)
    expert_hidden = (jax.nn.silu(projected[..., :hidden_width]) * projected[..., hidden_width:]).astype(jnp.bfloat16)
    expert_out = jnp.einsum("secf,efd->secd", expert_hidden, w_down, preferred_element_type=jnp.float32)
    produced = expert_out.astype(jnp.bfloat16).reshape(devices, -1, width)
    returned = lax.all_to_all(produced, axes, split_axis=0, concat_axis=0, tiled=True)
    picked = returned.reshape(-1, width)[slot_index].reshape(own_rows, TOP, width).astype(jnp.float32)
    return jnp.sum(picked * route_weight[:, :, None], axis=1)


def per_device(
    queries,
    cached,
    new_entries,
    lengths,
    residual,
    w_out,
    norm_gain,
    w_gate_up,
    w_down,
    routes,
    gate_codes,
    *,
    sheet,
):
    rows = residual.shape[1]
    groups = lax.axis_size("grp")
    me = lax.axis_index("grp")
    if sheet:
        mine = share_codes(routes[0], gate_codes[0])

    def attend(i):
        return attend_rows(
            jnp.stack([lengths[0], me ^ i]), queries[0, 0], cached[0, 0], new_entries[0, 0], w_out, rows,
            (jnp.bfloat16,),
        )[0]

    waiting = [[] for _ in range(groups)]
    bit = 1
    while bit < groups:
        for i in range(groups - bit, 0, -2 * bit):
            part = attend(i)
            if waiting[i]:
                part = sum((v.astype(jnp.float32) for v in waiting[i]), part.astype(jnp.float32)).astype(part.dtype)
            waiting[i - bit].append(swap(part, "grp", bit))
        bit *= 2
    own = attend(0)
    attn_out, state, normed = norm_rows(own, waiting[0], residual[0], norm_gain)
    if sheet:
        total = experts(spread(normed), *place_codes(mine), w_gate_up, w_down)
        moe_total = total / jnp.sum(gate_codes[0].astype(jnp.float32), axis=-1, keepdims=True)
    else:
        moe_total = moe_exchange(normed, routes[0], gate_codes[0], w_gate_up, w_down)
    mixed = (state + moe_total).astype(jnp.bfloat16)
    return (attn_out[None], mixed[None])


def solution(mesh):
    placed = (
        P("grp", ("sub", "dev"), None, None),
        P("grp", ("sub", "dev"), None, None),
        P("grp", ("sub", "dev"), None, None),
        P(("sub", "dev")),
        P(("sub", "dev"), "grp", None),
        P("grp", None),
        P(),
        P(("grp", "sub", "dev"), None, None),
        P(("grp", "sub", "dev"), None, None),
        P(("sub", "dev"), "grp", None),
        P(("sub", "dev"), "grp", None),
    )
    shape = mesh.shape
    sheet = shape["grp"] == 4 and shape["sub"] == 4 and shape["dev"] == 2

    def body(*args):
        return per_device(*args, sheet=sheet)

    return jax.shard_map(
        body,
        mesh=mesh,
        in_specs=placed,
        out_specs=(P(("sub", "dev"), "grp", None), P(("sub", "dev"), "grp", None)),
        check_vma=False,
    )
```
